512 devices in a mesh: dp: 8 (over x, core), expert: 64 (over z, y).
Axes of the slice: x: 4, y: 4, z: 16, core: 2. Of those that a mesh axis runs over, the one named last changes fastest.
Arguments:
- cells: bfloat16 [131072, 1024], P(('dp', 'expert')), may hold values from -6 to 6
- cell_bins: int32 [131072], P(('dp', 'expert')), may hold values from 0 to 127
- tile_counts: int32 [512, 8], P(('dp', 'expert')), may hold values from 1 to 96, 256 in all within a row
- bin_base: bfloat16 [65536, 1024], P(('dp', 'expert')), may hold values from -6 to 6
- norm_gain: float32 [1024], replicated, may hold values from 0.1 to 1.9
- expert_ids: int32 [65536, 1], P(('dp', 'expert')), may hold values from 0 to 63; in each aligned block of 128 rows (0 to 127, 128 to 255, ...) at most 3 rows name the same one
- gate_q: bfloat16 [64, 4096, 1024], P('expert', 'dp'), may hold values from -0.1875 to 0.1875
- up_q: bfloat16 [64, 4096, 1024], P('expert', 'dp'), may hold values from -0.1875 to 0.1875
- down_q: bfloat16 [64, 4096, 1024], P('expert', 'dp'), may hold values from -0.09375 to 0.09375
- gate_scales: int32 [64, 32, 8], P('expert', 'dp'), may hold values from -1 to 1
- up_scales: int32 [64, 32, 8], P('expert', 'dp'), may hold values from -1 to 1
- down_scales: int32 [64, 32, 8], P('expert', 'dp'), may hold values from -1 to 1
Outputs:
- encoded: bfloat16 [65536, 1024], P(('dp', 'expert'))
The draws below stay inside these ranges and needn't reach their ends.
Inputs may be any that keep to these rules, and one draw needn't show every extreme that they name: Each device's cells are stored grouped by tile in order of t; row s of tile_counts gives the lengths of these groups, sums to 256, and its largest entry is 96. `expert_ids`: among the 128 bins of one tile no expert is named more than 3 times, a bound that some block reaches.
All inputs are finite; a program needn't handle non-finite values.
Results may differ from the reference program's by a relative error of at most 0.014.
Values may be sent and summed in bfloat16 or wider, within the bound.
No kernel may reach another device: no remote copies, remote signals or barrier semaphores. Data moves between devices by JAX's collectives and lax.ppermute only.
A program may use at most 64 MiB of HBM per device.

```python
import math
import jax
import jax.numpy as jnp
import numpy as np
from jax import lax

D = 1024
FF = 4096
QB = 128
TOK_DEV = 128
EXPERTS = 64
CELLS_DEV = 256
CAP = 3
CCAP = 96
HBLK = 512
BINS = 65536
CELLS = 131072
N_DP = 8
N_EXPERT = 64


def set_ends(entries, rng, low, largest):
    index_at = [jax.random.randint(jax.random.fold_in(rng, axis), (), 0, length) for axis, length in enumerate(entries.shape)]
    widest = entries.shape.index(max(entries.shape))
    next_to = index_at[:widest] + [(index_at[widest] + 1) % entries.shape[widest]] + index_at[widest + 1:]
    return entries.at[tuple(index_at)].set(low).at[tuple(next_to)].set(largest)


def shard_levels(rng, extent, cuts, smallest, high):
    level = 1.0
    for dim, shards_of in cuts:
        draws = jax.random.uniform(jax.random.fold_in(jax.random.fold_in(rng, 6), dim), (shards_of,), jnp.float32, smallest / len(cuts), high / len(cuts))
        level = level * jnp.repeat(jnp.exp(draws), extent[dim] // shards_of).reshape((-1,) + (1,) * (len(extent) - 1 - dim))
    return level


def profile(count, total, most, slope):
    loads = [(1 << 20) // math.isqrt(rank ** slope) + 1 for rank in range(2, count + 1)]
    rest, counts = total - most - (count - 1), [1] * (count - 1)
    while rest > 0:
        candidates = [i for i in range(count - 1) if counts[i] < most]
        pool, left = sum([loads[i] for i in candidates]), rest
        for i in candidates:
            extra = min(most - counts[i], max(1, left * loads[i] // pool), rest)
            counts[i] = counts[i] + extra
            rest = rest - extra
    return np.array([most] + counts)


def ragged(own_key, amount, total, reach, lean):
    if amount == 2:
        one = jax.random.randint(own_key, (), max(1, total - reach), min(reach, total - 1) + 1)
        return jnp.stack([one, total - one])
    lengths = jnp.asarray(profile(amount, total, reach, lean), jnp.int32)
    couples = (amount - 1) // 2
    donor, taker = lengths[1:1 + 2 * couples:2], lengths[2:2 + 2 * couples:2]
    slack = jnp.minimum(donor - 1, reach - taker)
    moved = jax.random.randint(jax.random.fold_in(own_key, 1), (couples,), 0, 1 << 20) % (slack + 1)
    lengths = lengths.at[1:1 + 2 * couples:2].set(donor - moved).at[2:2 + 2 * couples:2].set(taker + moved)
    return lengths[jax.random.permutation(jax.random.fold_in(own_key, 2), amount)]


def routed_block(stream_key, own, number, rows, amount, top, bound, slope):
    ranking = jax.random.permutation(stream_key, amount)
    heavy_load, common = load_shares(amount, rows * top, bound, slope, True), load_shares(amount, rows * top, bound, slope, False)
    places = jnp.arange(amount)

    def named(sizes, offset_by):
        used = int((sizes > 0).sum())
        fixed = max(1, used // 4)
        moved = fixed + (places - fixed + offset_by * (used - fixed)) % max(1, amount - fixed)
        return jnp.zeros((amount,), jnp.int32).at[ranking[jnp.where(places < fixed, places, moved)]].set(jnp.asarray(sizes, jnp.int32))

    sizes = jnp.where(number % 4 == 0, named(heavy_load, number // 4), named(common, number - number // 4 - 1))
    mixed = jax.random.permutation(jax.random.fold_in(own, 3), amount)
    giver, taker = mixed[0:amount // 2 * 2:2], mixed[1:amount // 2 * 2:2]
    room = jnp.minimum(sizes[giver] - 1, bound - sizes[taker]) // 2
    room = jnp.where((giver == ranking[0]) | (taker == ranking[0]) | (sizes[taker] == 0), 0, jnp.maximum(room, 0))
    moved = jax.random.randint(jax.random.fold_in(own, 4), (amount // 2,), 0, 1 << 20) % (room + 1)
    sizes = sizes.at[giver].add(-moved).at[taker].add(moved)
    labels = jnp.searchsorted(jnp.cumsum(sizes), jnp.arange(rows * top), side="right").astype(jnp.int32)
    table = labels.reshape(top, rows).T
    table = table[jax.random.permutation(jax.random.fold_in(own, 1), rows)]
    offset_by = jax.random.randint(jax.random.fold_in(own, 2), (rows, 1), 0, top)
    return jnp.take_along_axis(table, (jnp.arange(top)[None, :] + offset_by) % top, axis=1)


def load_shares(number_of, total, reach, skew, full):
    portions = [(1 << 20) // math.isqrt(standing ** skew) + 1 for standing in range(1, number_of + 1)]
    largest = reach if full else min(reach, max(-(-total // number_of), total * portions[0] // sum(portions)))
    least = 1 if total - largest >= number_of - 1 else 0
    holding, surplus = [largest] + [least] * (number_of - 1), total - largest - least * (number_of - 1)
    while surplus > 0:
        free = [i for i in range(1, number_of) if holding[i] < largest] or [i for i in range(1, number_of) if holding[i] < reach]
        whole, remaining = sum([portions[i] for i in free]), surplus
        for i in free:
            extra = min(reach - holding[i], max(1, remaining * portions[i] // whole), surplus)
            holding[i] = holding[i] + extra
            surplus = surplus - extra
    return np.array(holding)


def scatter_about(stream_key, shape, deviation, limit, pieces=(), held_as=jnp.bfloat16):
    array = deviation * jax.random.normal(stream_key, shape, jnp.float32)
    if pieces:
        array = array * shard_levels(stream_key, shape, pieces, -0.22, 0.18)
    return jnp.clip(array, -limit, limit).astype(held_as)


def setup_inputs(seed: int = 0) -> dict:
    key_of = jax.random.split(jax.random.key(seed), 13)
    cells = scatter_about(key_of[0], (CELLS, D), 1.0, 6.0, ((0, 512),))
    cell_bins = set_ends(jax.random.randint(key_of[1], (CELLS,), 0, TOK_DEV), jax.random.fold_in(key_of[1], 1), 0, TOK_DEV - 1).astype(jnp.int32)
    tile_counts = jax.vmap(lambda own: ragged(own, N_DP, CELLS_DEV, CCAP, 2))(jax.random.split(key_of[2], (N_DP * N_EXPERT))).reshape((N_DP * N_EXPERT, N_DP)).astype(jnp.int32)
    bin_base = scatter_about(key_of[3], (BINS, D), 1.0, 6.0, ((0, 512),))
    norm_gain = jnp.clip(1.0 + 0.18 * jax.random.normal(key_of[4], (D,), jnp.float32), 0.1, 1.9)
    expert_ids_keys = jax.random.split(jax.random.fold_in(key_of[5], 1), BINS // TOK_DEV)
    expert_ids_turns = jax.random.permutation(jax.random.fold_in(key_of[5], 3), BINS // TOK_DEV)
    expert_ids = jax.vmap(lambda own, number: routed_block(jax.random.fold_in(key_of[5], 2), own, number, TOK_DEV, EXPERTS, 1, CAP, 2))(expert_ids_keys, expert_ids_turns).reshape((BINS, 1))
    gate_q = scatter_about(key_of[6], (EXPERTS, FF, D), D ** -0.5, 0.1875, ((0, 64), (1, 8)))
    up_q = scatter_about(key_of[7], (EXPERTS, FF, D), D ** -0.5, 0.1875, ((0, 64), (1, 8)))
    down_q = scatter_about(key_of[8], (EXPERTS, FF, D), FF ** -0.5, 0.09375, ((0, 64), (1, 8)))
    gate_scales = set_ends(jax.random.randint(key_of[9], (EXPERTS, FF // QB, D // QB), -1, 2), jax.random.fold_in(key_of[9], 1), -1, 1).astype(jnp.int32)
    up_scales = set_ends(jax.random.randint(key_of[10], (EXPERTS, FF // QB, D // QB), -1, 2), jax.random.fold_in(key_of[10], 1), -1, 1).astype(jnp.int32)
    down_scales = set_ends(jax.random.randint(key_of[11], (EXPERTS, FF // QB, D // QB), -1, 2), jax.random.fold_in(key_of[11], 1), -1, 1).astype(jnp.int32)
    return dict(cells=cells, cell_bins=cell_bins, tile_counts=tile_counts, bin_base=bin_base, norm_gain=norm_gain, expert_ids=expert_ids, gate_q=gate_q, up_q=up_q, down_q=down_q, gate_scales=gate_scales, up_scales=up_scales, down_scales=down_scales)


def dequantize(quant, scale):
    factor = jnp.exp2(scale.astype(jnp.float32))
    factor = jnp.repeat(jnp.repeat(factor, QB, axis=0), QB, axis=1).astype(jnp.bfloat16)
    return quant * factor

def reference(cells, cell_bins, tile_counts, bin_base, norm_gain, expert_ids, gate_q, up_q, down_q, gate_scales, up_scales, down_scales):
    n_devices = N_DP * N_EXPERT
    cell_pos = jnp.arange(CELLS_DEV, dtype=jnp.int32)
    run_ends = jnp.cumsum(tile_counts, axis=1).astype(jnp.int32)
    dest_tile = lax.optimization_barrier(jnp.sum((cell_pos[None, :, None] >= run_ends[:, None, :]).astype(jnp.int32), axis=2))
    source = jnp.arange(n_devices, dtype=jnp.int32)
    dest_dev = dest_tile * N_EXPERT + (source % N_EXPERT)[:, None]
    bin_index = (dest_dev * TOK_DEV + cell_bins.reshape(n_devices, CELLS_DEV)).reshape(-1).astype(jnp.int32)
    splat_sum = jax.ops.segment_sum(cells.astype(jnp.float32), bin_index, num_segments=BINS)
    residual_in = bin_base.astype(jnp.float32) + splat_sum
    mean_sq = lax.optimization_barrier(jnp.mean(residual_in * residual_in, axis=1, keepdims=True))
    normed = (residual_in * lax.rsqrt(mean_sq + 1e-06) * norm_gain[None, :]).astype(jnp.bfloat16)
    expert_col = expert_ids[:, 0].reshape(n_devices, TOK_DEV)
    one_hot = (expert_col[:, :, None] == jnp.arange(EXPERTS, dtype=jnp.int32)[None, None, :]).astype(jnp.int32)
    within = lax.optimization_barrier(jnp.sum(jnp.cumsum(one_hot, axis=1) * one_hot, axis=2)) - 1
    row_of = (source[:, None] * CAP + within).reshape(-1).astype(jnp.int32)
    expert_flat = expert_col.reshape(-1).astype(jnp.int32)
    buffer = jnp.zeros((EXPERTS, n_devices * CAP, D), jnp.bfloat16).at[expert_flat, row_of].set(normed)

    def expert_ffn(operands):
        rows_in, gq, uq, dq, gs, us, ds = operands
        w_gate = dequantize(gq, gs)
        w_up = dequantize(uq, us)
        w_down = dequantize(dq, ds)
        contract = (((1,), (1,)), ((), ()))
        gate_val = lax.dot_general(rows_in, w_gate, contract, preferred_element_type=jnp.float32)
        up_val = lax.dot_general(rows_in, w_up, contract, preferred_element_type=jnp.float32)
        hidden = (jax.nn.silu(gate_val) * up_val).astype(jnp.bfloat16)
        summed = jnp.zeros((rows_in.shape[0], D), jnp.float32)
        for block in range(N_DP):
            partial_value = jnp.dot(hidden[:, block * HBLK:(block + 1) * HBLK], w_down[block * HBLK:(block + 1) * HBLK, :], preferred_element_type=jnp.float32).astype(jnp.bfloat16)
            partial_value = lax.optimization_barrier(partial_value)
            summed = summed + partial_value.astype(jnp.float32)
        return summed.astype(jnp.bfloat16)
    results = lax.map(expert_ffn, (buffer, gate_q, up_q, down_q, gate_scales, up_scales, down_scales))
    expert_out = results[expert_flat, row_of].astype(jnp.float32)
    return (residual_in + expert_out).astype(jnp.bfloat16)
```

```python
import functools

import jax
import jax.numpy as jnp
from jax import lax
from jax.experimental import pallas as pl
from jax.experimental.pallas import tpu as pltpu
from jax.sharding import PartitionSpec as P

QB = 128
CORES = 2


def dequant_kernel(gs, us, ds, gq, uq, dq, gw, uw, dw):
    row = pl.program_id(0)
    for s_ref, q_ref, w_ref in ((gs, gq, gw), (us, uq, uw), (ds, dq, dw)):
        for col in range(q_ref.shape[1] // QB):
            span = slice(col * QB, (col + 1) * QB)
            factor = jnp.exp2(jnp.full((QB, QB), s_ref[row, col], jnp.int32).astype(jnp.float32))
            w_ref[:, span] = q_ref[:, span] * factor.astype(jnp.bfloat16)


def dequantize_all(quants, scales):
    rows, cols = quants[0].shape
    block = pl.BlockSpec((QB, cols), lambda r: (r, 0))
    return pl.pallas_call(
        dequant_kernel,
        grid=(rows // QB,),
        in_specs=[pl.BlockSpec(memory_space=pltpu.SMEM)] * 3 + [block] * 3,
        out_specs=[block] * 3,
        out_shape=[jax.ShapeDtypeStruct((rows, cols), jnp.bfloat16)] * 3,
        name="dequantize",
    )(*scales, *quants)


def ffn_kernel(x_ref, *refs):
    weights, out_ref, total = refs[:6], refs[6], refs[7]
    contract = (((1,), (1,)), ((), ()))
    x = x_ref[...]
    part = jnp.zeros(total.shape, jnp.float32)
    for half in range(2):
        gate_w, up_w, down_w = weights[3 * half : 3 * half + 3]
        gate = lax.dot_general(x, gate_w[...], contract, preferred_element_type=jnp.float32)
        up = lax.dot_general(x, up_w[...], contract, preferred_element_type=jnp.float32)
        hidden = (gate / (1.0 + jnp.exp(-gate)) * up).astype(jnp.bfloat16)
        part = part + jnp.dot(hidden, down_w[...], preferred_element_type=jnp.float32)
    step = pl.program_id(0)

    @pl.when(step == 0)
    def _():
        total[...] = part

    @pl.when(step > 0)
    def _():
        total[...] += part

    @pl.when(step == pl.num_programs(0) - 1)
    def _():
        out_ref[...] = total[...].astype(out_ref.dtype)


def ffn(x, mine, theirs, chunk=256):
    rows, width = x.shape
    hidden = mine[0].shape[0]
    block = pl.BlockSpec((chunk, width), lambda h: (h, 0))
    whole = pl.BlockSpec((rows, width), lambda h: (0, 0))
    return pl.pallas_call(
        ffn_kernel,
        grid=(hidden // chunk,),
        in_specs=[whole] + [block] * 6,
        out_specs=whole,
        out_shape=jax.ShapeDtypeStruct((rows, width), jnp.bfloat16),
        scratch_shapes=[pltpu.VMEM((rows, width), jnp.float32)],
        compiler_params=pltpu.CompilerParams(vmem_limit_bytes=40 << 20),
        name="ffn",
    )(x, *mine, *theirs)


def on_device(
    cells,
    cell_bins,
    tile_counts,
    bin_base,
    norm_gain,
    expert_ids,
    gate_q,
    up_q,
    down_q,
    gate_scales,
    up_scales,
    down_scales,
):
    dp_size = lax.axis_size("dp")
    chips = dp_size // CORES
    expert_count = lax.axis_size("expert") * gate_q.shape[0]
    cell_total, width = cells.shape
    tile_bins = bin_base.shape[0]
    core = lax.axis_index("dp") % CORES
    to_core = [(i, i ^ 1) for i in range(dp_size)]

    def to_chip(k):
        return [(i, (i + CORES * k) % dp_size) for i in range(dp_size)]

    same_core = [[CORES * x + c for x in range(chips)] for c in range(CORES)]

    other_cells = lax.ppermute(cells, "dp", to_core)
    ends = jnp.cumsum(tile_counts[0])
    tile_of = jnp.sum(
        (jnp.arange(cell_total, dtype=jnp.int32)[None, :] >= ends[:, None]).astype(jnp.int32), axis=0
    )
    code = tile_of * tile_bins + cell_bins
    other_code = lax.ppermute(code, "dp", to_core)
    row = jnp.arange(chips * tile_bins, dtype=jnp.int32)
    wanted = (row // tile_bins * CORES + core) * tile_bins + row % tile_bins
    sums = jnp.dot(
        (wanted[:, None] == code[None, :]).astype(jnp.bfloat16), cells, preferred_element_type=jnp.float32
    ) + jnp.dot(
        (wanted[:, None] == other_code[None, :]).astype(jnp.bfloat16),
        other_cells,
        preferred_element_type=jnp.float32,
    )
    sums = sums.astype(jnp.bfloat16).reshape(chips, tile_bins, width)
    weights = dequantize_all(
        (gate_q[0], up_q[0], down_q[0]), (gate_scales[0], up_scales[0], down_scales[0])
    )
    *weights, sums = lax.optimization_barrier((*weights, sums))
    got = lax.all_to_all(
        sums, "dp", split_axis=0, concat_axis=0, tiled=True, axis_index_groups=same_core
    )
    other_weights = [lax.ppermute(w, "dp", to_core) for w in weights]
    residual_in = bin_base.astype(jnp.float32) + jnp.sum(got.astype(jnp.float32), axis=0)
    mean_sq = jnp.mean(residual_in * residual_in, axis=1, keepdims=True)
    normed = (residual_in * lax.rsqrt(mean_sq + 1e-06) * norm_gain[None, :]).astype(jnp.bfloat16)

    capacity = max(2, 3 * tile_bins // (2 * expert_count))
    expert_col = expert_ids[:, 0]
    one_hot = (expert_col[:, None] == jnp.arange(expert_count, dtype=jnp.int32)[None, :]).astype(
        jnp.int32
    )
    within = jnp.sum(jnp.cumsum(one_hot, axis=0) * one_hot, axis=1) - 1
    slot_of = expert_col * capacity + within
    slots = expert_count * capacity
    placer = (jnp.arange(slots, dtype=jnp.int32)[:, None] == slot_of[None, :]).astype(jnp.bfloat16)
    outgoing = jnp.dot(placer, normed, preferred_element_type=jnp.float32).astype(jnp.bfloat16)
    dense = (expert_count, capacity * width // QB, QB)
    arrived = lax.all_to_all(
        outgoing.reshape(dense), "expert", split_axis=0, concat_axis=0, tiled=True
    ).reshape(slots, width)

    others = [lax.ppermute(arrived, "dp", to_chip(k)) for k in range(1, chips)]
    total = ffn(arrived, weights, other_weights).astype(jnp.float32)
    for k, rows in enumerate(others, 1):
        back = lax.ppermute(ffn(rows, weights, other_weights), "dp", to_chip(chips - k))
        total = total + back.astype(jnp.float32)
    returned = lax.all_to_all(
        total.astype(jnp.bfloat16).reshape(dense), "expert", split_axis=0, concat_axis=0, tiled=True
    ).reshape(slots, width)
    expert_out = lax.dot_general(
        placer, returned, (((0,), (0,)), ((), ())), preferred_element_type=jnp.float32
    )
    return (residual_in + expert_out).astype(jnp.bfloat16)


def solution(mesh):
    split = P(("dp", "expert"), None)
    placed = (split, P(("dp", "expert")), split, split, P(), split) + (P("expert", "dp", None),) * 6
    return jax.shard_map(on_device, mesh=mesh, in_specs=placed, out_specs=split, check_vma=False)
```

```python
import jax
import jax.numpy as jnp
from jax import lax
from jax.experimental import pallas as pl
from jax.experimental.pallas import tpu as pltpu
from jax.sharding import PartitionSpec as P

QB = 128
CORES = 2
CHUNK = 256
LIMIT = 8 << 20


def in_vmem(x):
    return pltpu.with_memory_space_constraint(x, pltpu.VMEM)


def in_hbm(x):
    return pltpu.with_memory_space_constraint(x, pltpu.HBM)


def code_kernel(counts_ref, bins_ref, code_ref):
    total = bins_ref.shape[1]
    position = lax.broadcasted_iota(jnp.int32, (1, total), 1)
    tile = jnp.zeros((1, total), jnp.int32)
    run_end = jnp.int32(0)
    for k in range(counts_ref.shape[1]):
        run_end = run_end + counts_ref[0, k]
        tile = tile + (position >= run_end).astype(jnp.int32)
    code_ref[...] = tile * QB + bins_ref[...]


def codes(counts, bins):
    return pl.pallas_call(
        code_kernel,
        in_specs=[pl.BlockSpec(memory_space=pltpu.SMEM), pl.BlockSpec(memory_space=pltpu.VMEM)],
        out_specs=pl.BlockSpec(memory_space=pltpu.VMEM),
        out_shape=pltpu.VMEM(bins.shape, jnp.int32),
        compiler_params=pltpu.CompilerParams(vmem_limit_bytes=LIMIT),
        name="codes",
    )(in_hbm(counts), in_hbm(bins))


def splat_kernel(core_ref, code_ref, other_code_ref, cells_ref, other_cells_ref, out_ref, held, sem):
    copy = pltpu.make_async_copy(cells_ref, held, sem)
    copy.start()
    chips, rows, _ = out_ref.shape
    row = lax.broadcasted_iota(jnp.int32, (chips, rows, held.shape[0]), 1)
    chip = lax.broadcasted_iota(jnp.int32, (chips, rows, held.shape[0]), 0)
    bins = ((chip * CORES + core_ref[0]) * rows + row).reshape(chips * rows, held.shape[0])

    def summed(its_code, its_cells):
        match = (bins == its_code[...]).astype(jnp.float32).astype(jnp.bfloat16)
        return jnp.dot(match, its_cells[...], preferred_element_type=jnp.float32)

    total = summed(other_code_ref, other_cells_ref)
    copy.wait()
    total = total + summed(code_ref, held)
    out_ref[...] = total.astype(out_ref.dtype).reshape(out_ref.shape)


def splat(core, code, other_code, cells, other_cells, chips, tile_bins):
    vmem = pl.BlockSpec(memory_space=pltpu.VMEM)
    return pl.pallas_call(
        splat_kernel,
        in_specs=[pl.BlockSpec(memory_space=pltpu.SMEM), vmem, vmem, pl.BlockSpec(memory_space=pl.ANY), vmem],
        out_specs=vmem,
        out_shape=pltpu.VMEM((chips, tile_bins, cells.shape[1]), jnp.bfloat16),
        scratch_shapes=[pltpu.VMEM(cells.shape, jnp.bfloat16), pltpu.SemaphoreType.DMA],
        compiler_params=pltpu.CompilerParams(vmem_limit_bytes=LIMIT),
        name="splat",
    )(core, in_vmem(code), in_vmem(other_code), in_hbm(cells), in_vmem(other_cells))


def dequant_kernel(gs, us, ds, gq, uq, dq, *outs):
    hidden, width = gq.shape

    def scaled(s_ref, q_ref, row, col):
        block = q_ref[row * QB : (row + 1) * QB, col * QB : (col + 1) * QB]
        exponent = jnp.full((1, QB), s_ref[row, col], jnp.int32)
        return block * jnp.exp2(exponent.astype(jnp.float32)).astype(jnp.bfloat16)

    for row in range(hidden // QB):
        out, at = outs[row * QB // CHUNK], row * QB % CHUNK
        for col in range(width // QB):
            rows, cols = slice(row * QB, (row + 1) * QB), slice(col * QB, (col + 1) * QB)
            out[cols, at : at + QB] = scaled(gs, gq, row, col).T
            out[cols, CHUNK + at : CHUNK + at + QB] = scaled(us, uq, row, col).T
            outs[-1][rows, cols] = scaled(ds, dq, row, col)


def dequantize_all(quants, scales):
    rows, cols = quants[0].shape
    vmem = pl.BlockSpec(memory_space=pltpu.VMEM)
    chunks = rows // CHUNK
    return pl.pallas_call(
        dequant_kernel,
        in_specs=[pl.BlockSpec(memory_space=pltpu.SMEM)] * 3 + [vmem] * 3,
        out_specs=[vmem] * (chunks + 1),
        out_shape=[pltpu.HBM((cols, 2 * CHUNK), jnp.bfloat16)] * chunks
        + [pltpu.HBM((rows, cols), jnp.bfloat16)],
        compiler_params=pltpu.CompilerParams(vmem_limit_bytes=LIMIT),
        name="dequantize",
    )(*scales, *quants)


def route_kernel(got_ref, base_ref, gain_ref, slot_ref, out_ref, residual_ref, spread, kept, sem):
    residual = base_ref[...].astype(jnp.float32)
    for chip in range(got_ref.shape[0]):
        residual = residual + got_ref[chip].astype(jnp.float32)
    kept[...] = residual
    copy = pltpu.make_async_copy(kept, residual_ref, sem)
    copy.start()
    mean_sq = jnp.mean(residual * residual, axis=1, keepdims=True)
    normed = (residual * lax.rsqrt(mean_sq + 1e-06) * gain_ref[...]).astype(jnp.bfloat16)
    bins, width = residual.shape
    slots = out_ref.shape[0] * QB // width
    placer = lax.broadcasted_iota(jnp.int32, (slots, bins), 0) == slot_ref[...]
    placed = jnp.dot(
        placer.astype(jnp.float32).astype(jnp.bfloat16), normed, preferred_element_type=jnp.float32
    )
    spread_rows(placed, spread, out_ref)
    copy.wait()


def route(got, base, gain, slot_of, slots):
    bins, width = base.shape
    rows = slots * width // QB
    vmem = pl.BlockSpec(memory_space=pltpu.VMEM)
    return pl.pallas_call(
        route_kernel,
        in_specs=[vmem] * 4,
        out_specs=[vmem, pl.BlockSpec(memory_space=pltpu.HBM)],
        out_shape=[
            pltpu.VMEM((rows, QB), jnp.bfloat16),
            pltpu.HBM((bins, width), jnp.float32),
        ],
        scratch_shapes=[
            pltpu.VMEM((rows, QB), jnp.float32),
            pltpu.VMEM((bins, width), jnp.float32),
            pltpu.SemaphoreType.DMA,
        ],
        compiler_params=pltpu.CompilerParams(vmem_limit_bytes=LIMIT),
        name="route",
    )(in_vmem(got), in_vmem(base), gain, slot_of)


def through_experts(x, weights, wait=None):
    half = len(weights) // 2
    total = None
    for core in range(2):
        first, last = core * half, core * half + half - 1
        for i in range(first, last):
            if wait is not None:
                wait(i)
            both = jnp.dot(x, weights[i][...], preferred_element_type=jnp.float32)
            gate, up = both[:, :CHUNK], both[:, CHUNK:]
            hidden = (gate / (1.0 + jnp.exp(-gate)) * up).astype(jnp.bfloat16)
            if wait is not None and i == first:
                wait(last)
            at = (i - first) * CHUNK
            part = jnp.dot(hidden, weights[last][at : at + CHUNK, :], preferred_element_type=jnp.float32)
            total = part if total is None else total + part
    return total


def load_ffn_kernel(x_ref, *refs):
    count = (len(refs) - 2) // 2
    weights, out_ref, held, sems = refs[:count], refs[count], refs[count + 1 : -1], refs[-1]
    copies = [pltpu.make_async_copy(weights[i], held[i], sems.at[i]) for i in range(count)]
    for copy in copies:
        copy.start()
    out_ref[...] = through_experts(x_ref[...], held, lambda i: copies[i].wait()).astype(out_ref.dtype)


def load_ffn(x, weights):
    vmem = pl.BlockSpec(memory_space=pltpu.VMEM)
    hbm = pl.BlockSpec(memory_space=pltpu.HBM)
    out, *held = pl.pallas_call(
        load_ffn_kernel,
        in_specs=[vmem] + [hbm] * len(weights),
        out_specs=[vmem] * (1 + len(weights)),
        out_shape=[pltpu.VMEM(v.shape, jnp.bfloat16) for v in (x, *weights)],
        scratch_shapes=[pltpu.SemaphoreType.DMA((len(weights),))],
        compiler_params=pltpu.CompilerParams(vmem_limit_bytes=LIMIT),
        name="load_ffn",
    )(in_vmem(x), *(in_hbm(w) for w in weights))
    return out, held


def ffn_kernel(x_ref, *refs):
    *weights, out_ref = refs
    out_ref[...] = through_experts(x_ref[...], weights).astype(out_ref.dtype)


def ffn(x, weights):
    vmem = pl.BlockSpec(memory_space=pltpu.VMEM)
    return pl.pallas_call(
        ffn_kernel,
        in_specs=[vmem] * (1 + len(weights)),
        out_specs=vmem,
        out_shape=pltpu.VMEM(x.shape, jnp.bfloat16),
        compiler_params=pltpu.CompilerParams(vmem_limit_bytes=LIMIT),
        name="ffn",
    )(*(in_vmem(v) for v in (x, *weights)))


def spread_rows(rows, spread, out_ref):
    lanes = rows.shape[1] // QB
    for col in range(lanes):
        spread[pl.ds(col, rows.shape[0], stride=lanes), :] = rows[:, col * QB : (col + 1) * QB]
    out_ref[...] = spread[...].astype(out_ref.dtype)


def combine_kernel(*refs):
    *parts, out_ref, spread = refs
    total = parts[0][...].astype(jnp.float32)
    for part in parts[1:]:
        total = total + part[...].astype(jnp.float32)
    spread_rows(total, spread, out_ref)


def combine(parts):
    slots, width = parts[0].shape
    vmem = pl.BlockSpec(memory_space=pltpu.VMEM)
    rows = slots * width // QB
    return pl.pallas_call(
        combine_kernel,
        in_specs=[vmem] * len(parts),
        out_specs=vmem,
        out_shape=pltpu.VMEM((rows, QB), jnp.bfloat16),
        scratch_shapes=[pltpu.VMEM((rows, QB), jnp.float32)],
        compiler_params=pltpu.CompilerParams(vmem_limit_bytes=LIMIT),
        name="combine",
    )(*(in_vmem(part) for part in parts))


def on_device(
    cells,
    cell_bins,
    tile_counts,
    bin_base,
    norm_gain,
    expert_ids,
    gate_q,
    up_q,
    down_q,
    gate_scales,
    up_scales,
    down_scales,
):
    dp_size = lax.axis_size("dp")
    chips = dp_size // CORES
    expert_count = lax.axis_size("expert") * gate_q.shape[0]
    cell_total, width = cells.shape
    tile_bins = bin_base.shape[0]
    core = (lax.axis_index("dp") % CORES).astype(jnp.int32).reshape(1)
    to_core = [(i, i ^ 1) for i in range(dp_size)]

    def to_chip(k):
        return [(i, (i + CORES * k) % dp_size) for i in range(dp_size)]

    same_core = [[CORES * x + c for x in range(chips)] for c in range(CORES)]

    other_cells = lax.ppermute(cells, "dp", to_core)
    code = codes(tile_counts, cell_bins.reshape(1, cell_total))
    other_code = lax.ppermute(code, "dp", to_core)
    sums = splat(core, code, other_code, cells, other_cells, chips, tile_bins)
    quants = (gate_q[0], up_q[0], down_q[0])
    *quants, sums = lax.optimization_barrier((*quants, sums))
    got = lax.all_to_all(
        sums,
        "dp",
        split_axis=0,
        concat_axis=0,
        tiled=True,
        axis_index_groups=same_core,
    )
    mine = dequantize_all(quants, (gate_scales[0], up_scales[0], down_scales[0]))
    theirs = [lax.ppermute(w, "dp", to_core) for w in mine]

    capacity = max(2, 3 * tile_bins // (2 * expert_count))
    expert_col = expert_ids[:, 0]
    one_hot = (expert_col[:, None] == jnp.arange(expert_count, dtype=jnp.int32)[None, :]).astype(
        jnp.int32
    )
    within = jnp.sum(jnp.cumsum(one_hot, axis=0) * one_hot, axis=1) - 1
    slot_of = expert_col * capacity + within
    slots = expert_count * capacity
    outgoing, residual_in = route(
        got, bin_base, norm_gain.reshape(1, width), slot_of.reshape(1, tile_bins), slots
    )
    dense = (expert_count, capacity * width // QB, QB)
    arrived = lax.all_to_all(
        outgoing.reshape(dense), "expert", split_axis=0, concat_axis=0, tiled=True
    ).reshape(slots, width)

    others = [(k, lax.ppermute(arrived, "dp", to_chip(k))) for k in (1, chips - 1, *range(2, chips - 1))]
    own, held = load_ffn(arrived, [*mine, *theirs])
    backs = [lax.ppermute(ffn(there, held), "dp", to_chip(chips - k)) for k, there in others]
    returned = lax.all_to_all(
        combine([own, *backs]).reshape(dense), "expert", split_axis=0, concat_axis=0, tiled=True
    ).reshape(slots, width)
    placer = (jnp.arange(slots, dtype=jnp.int32)[:, None] == slot_of[None, :]).astype(jnp.bfloat16)
    expert_out = lax.dot_general(
        placer, returned, (((0,), (0,)), ((), ())), preferred_element_type=jnp.float32
    )
    return (residual_in + expert_out).astype(jnp.bfloat16)


def solution(mesh):
    split = P(("dp", "expert"), None)
    placed = (split, P(("dp", "expert")), split, split, P(), split) + (P("expert", "dp", None),) * 6
    return jax.shard_map(on_device, mesh=mesh, in_specs=placed, out_specs=split, check_vma=False)
```

```python
import jax
import jax.numpy as jnp
from jax import lax
from jax.experimental import pallas as pl
from jax.experimental.pallas import tpu as pltpu
from jax.sharding import PartitionSpec as P

QB = 128
CORES = 2
CHUNK = 256
LIMIT = 8 << 20


def in_vmem(x):
    return pltpu.with_memory_space_constraint(x, pltpu.VMEM)


def in_hbm(x):
    return pltpu.with_memory_space_constraint(x, pltpu.HBM)


def splat_kernel(counts_ref, core_ref, bins_ref, cells_ref, other_ref, own_ref, held, sem):
    copy = pltpu.make_async_copy(cells_ref, held, sem)
    copy.start()
    chips, rows, _ = own_ref.shape
    total = held.shape[0]
    position = lax.broadcasted_iota(jnp.int32, (1, total), 1)
    tile = jnp.zeros((1, total), jnp.int32)
    run_end = jnp.int32(0)
    for k in range(counts_ref.shape[1]):
        run_end = run_end + counts_ref[0, k]
        tile = tile + (position >= run_end).astype(jnp.int32)
    code = tile * rows + bins_ref[...]
    row = lax.broadcasted_iota(jnp.int32, (rows, total), 0)
    copy.wait()
    cells = held[...]
    for core, out_ref in ((1 - core_ref[0], other_ref), (core_ref[0], own_ref)):
        for chip in range(chips):
            match = row + (chip * CORES + core) * rows == code
            out_ref[chip] = jnp.dot(
                match.astype(jnp.float32).astype(jnp.bfloat16), cells, preferred_element_type=jnp.float32
            ).astype(out_ref.dtype)


def splat(counts, core, bins, cells, chips, tile_bins):
    vmem = pl.BlockSpec(memory_space=pltpu.VMEM)
    smem = pl.BlockSpec(memory_space=pltpu.SMEM)
    shape = (chips, tile_bins, cells.shape[1])
    return pl.pallas_call(
        splat_kernel,
        in_specs=[smem, smem, vmem, pl.BlockSpec(memory_space=pltpu.HBM)],
        out_specs=[vmem, vmem],
        out_shape=[pltpu.VMEM(shape, jnp.bfloat16), pltpu.VMEM(shape, jnp.float32)],
        scratch_shapes=[pltpu.VMEM(cells.shape, jnp.bfloat16), pltpu.SemaphoreType.DMA],
        compiler_params=pltpu.CompilerParams(vmem_limit_bytes=LIMIT),
        name="splat",
    )(in_hbm(counts), core, in_hbm(bins), in_hbm(cells))


def join_kernel(own_ref, got_ref, out_ref, sums, sems):
    chips = own_ref.shape[0]
    copies = [pltpu.make_async_copy(sums.at[chip], out_ref.at[chip], sems.at[chip]) for chip in range(chips)]
    for chip in range(chips):
        sums[chip] = (own_ref[chip] + got_ref[chip].astype(jnp.float32)).astype(sums.dtype)
        copies[chip].start()
    for copy in copies:
        copy.wait()


def join(own, got):
    vmem = pl.BlockSpec(memory_space=pltpu.VMEM)
    return pl.pallas_call(
        join_kernel,
        in_specs=[vmem, vmem],
        out_specs=pl.BlockSpec(memory_space=pltpu.HBM),
        out_shape=pltpu.HBM(got.shape, got.dtype),
        scratch_shapes=[pltpu.VMEM(got.shape, got.dtype), pltpu.SemaphoreType.DMA((got.shape[0],))],
        compiler_params=pltpu.CompilerParams(vmem_limit_bytes=LIMIT),
        name="join",
    )(in_vmem(own), in_vmem(got))


def dequant_kernel(gs, us, ds, gq, uq, dq, *outs):
    hidden, width = gq.shape

    def scaled(s_ref, q_ref, row, col):
        block = q_ref[row * QB : (row + 1) * QB, col * QB : (col + 1) * QB]
        exponent = jnp.full((1, QB), s_ref[row, col], jnp.int32)
        return block * jnp.exp2(exponent.astype(jnp.float32)).astype(jnp.bfloat16)

    for row in range(hidden // QB):
        out, at = outs[row * QB // CHUNK], row * QB % CHUNK
        for col in range(width // QB):
            rows, cols = slice(row * QB, (row + 1) * QB), slice(col * QB, (col + 1) * QB)
            out[cols, at : at + QB] = scaled(gs, gq, row, col).T
            out[cols, CHUNK + at : CHUNK + at + QB] = scaled(us, uq, row, col).T
            outs[-1][rows, cols] = scaled(ds, dq, row, col)


def dequantize_all(quants, scales):
    rows, cols = quants[0].shape
    vmem = pl.BlockSpec(memory_space=pltpu.VMEM)
    chunks = rows // CHUNK
    return pl.pallas_call(
        dequant_kernel,
        in_specs=[pl.BlockSpec(memory_space=pltpu.SMEM)] * 3 + [vmem] * 3,
        out_specs=[vmem] * (chunks + 1),
        out_shape=[pltpu.HBM((cols, 2 * CHUNK), jnp.bfloat16)] * chunks
        + [pltpu.HBM((rows, cols), jnp.bfloat16)],
        compiler_params=pltpu.CompilerParams(vmem_limit_bytes=LIMIT),
        name="dequantize",
    )(*scales, *quants)


def route_kernel(got_ref, base_ref, gain_ref, slot_ref, out_ref, residual_ref, spread, kept, sem):
    residual = base_ref[...].astype(jnp.float32)
    for chip in range(got_ref.shape[0]):
        residual = residual + got_ref[chip].astype(jnp.float32)
    kept[...] = residual
    copy = pltpu.make_async_copy(kept, residual_ref, sem)
    copy.start()
    mean_sq = jnp.mean(residual * residual, axis=1, keepdims=True)
    normed = (residual * lax.rsqrt(mean_sq + 1e-06) * gain_ref[...]).astype(jnp.bfloat16)
    bins, width = residual.shape
    slots = out_ref.shape[0] * QB // width
    placer = lax.broadcasted_iota(jnp.int32, (slots, bins), 0) == slot_ref[...]
    placed = jnp.dot(
        placer.astype(jnp.float32).astype(jnp.bfloat16), normed, preferred_element_type=jnp.float32
    )
    spread_rows(placed, spread, out_ref)
    copy.wait()


def route(got, base, gain, slot_of, slots):
    bins, width = base.shape
    rows = slots * width // QB
    vmem = pl.BlockSpec(memory_space=pltpu.VMEM)
    return pl.pallas_call(
        route_kernel,
        in_specs=[vmem] * 4,
        out_specs=[vmem, pl.BlockSpec(memory_space=pltpu.HBM)],
        out_shape=[
            pltpu.VMEM((rows, QB), jnp.bfloat16),
            pltpu.HBM((bins, width), jnp.float32),
        ],
        scratch_shapes=[
            pltpu.VMEM((rows, QB), jnp.float32),
            pltpu.VMEM((bins, width), jnp.float32),
            pltpu.SemaphoreType.DMA,
        ],
        compiler_params=pltpu.CompilerParams(vmem_limit_bytes=LIMIT),
        name="route",
    )(in_vmem(got), in_vmem(base), gain, slot_of)


def through_experts(x, weights, wait=None):
    half = len(weights) // 2
    total = None
    for core in range(2):
        first, last = core * half, core * half + half - 1
        for i in range(first, last):
            if wait is not None:
                wait(i)
            both = jnp.dot(x, weights[i][...], preferred_element_type=jnp.float32)
            gate, up = both[:, :CHUNK], both[:, CHUNK:]
            hidden = (gate / (1.0 + jnp.exp(-gate)) * up).astype(jnp.bfloat16)
            if wait is not None and i == first:
                wait(last)
            at = (i - first) * CHUNK
            part = jnp.dot(hidden, weights[last][at : at + CHUNK, :], preferred_element_type=jnp.float32)
            total = part if total is None else total + part
    return total


def load_ffn_kernel(x_ref, *refs):
    count = (len(refs) - 2) // 2
    weights, out_ref, held, sems = refs[:count], refs[count], refs[count + 1 : -1], refs[-1]
    copies = [pltpu.make_async_copy(weights[i], held[i], sems.at[i]) for i in range(count)]
    for copy in copies:
        copy.start()
    out_ref[...] = through_experts(x_ref[...], held, lambda i: copies[i].wait()).astype(out_ref.dtype)


def load_ffn(x, weights):
    vmem = pl.BlockSpec(memory_space=pltpu.VMEM)
    hbm = pl.BlockSpec(memory_space=pltpu.HBM)
    out, *held = pl.pallas_call(
        load_ffn_kernel,
        in_specs=[vmem] + [hbm] * len(weights),
        out_specs=[vmem] * (1 + len(weights)),
        out_shape=[pltpu.VMEM(v.shape, jnp.bfloat16) for v in (x, *weights)],
        scratch_shapes=[pltpu.SemaphoreType.DMA((len(weights),))],
        compiler_params=pltpu.CompilerParams(vmem_limit_bytes=LIMIT),
        name="load_ffn",
    )(in_vmem(x), *(in_hbm(w) for w in weights))
    return out, held


def ffn_kernel(x_ref, *refs):
    *weights, out_ref = refs
    out_ref[...] = through_experts(x_ref[...], weights).astype(out_ref.dtype)


def ffn(x, weights):
    vmem = pl.BlockSpec(memory_space=pltpu.VMEM)
    return pl.pallas_call(
        ffn_kernel,
        in_specs=[vmem] * (1 + len(weights)),
        out_specs=vmem,
        out_shape=pltpu.VMEM(x.shape, jnp.bfloat16),
        compiler_params=pltpu.CompilerParams(vmem_limit_bytes=LIMIT),
        name="ffn",
    )(*(in_vmem(v) for v in (x, *weights)))


def spread_rows(rows, spread, out_ref):
    lanes = rows.shape[1] // QB
    for col in range(lanes):
        spread[pl.ds(col, rows.shape[0], stride=lanes), :] = rows[:, col * QB : (col + 1) * QB]
    out_ref[...] = spread[...].astype(out_ref.dtype)


def combine_kernel(*refs):
    *parts, out_ref, spread = refs
    total = parts[0][...].astype(jnp.float32)
    for part in parts[1:]:
        total = total + part[...].astype(jnp.float32)
    spread_rows(total, spread, out_ref)


def combine(parts):
    slots, width = parts[0].shape
    vmem = pl.BlockSpec(memory_space=pltpu.VMEM)
    rows = slots * width // QB
    return pl.pallas_call(
        combine_kernel,
        in_specs=[vmem] * len(parts),
        out_specs=vmem,
        out_shape=pltpu.VMEM((rows, QB), jnp.bfloat16),
        scratch_shapes=[pltpu.VMEM((rows, QB), jnp.float32)],
        compiler_params=pltpu.CompilerParams(vmem_limit_bytes=LIMIT),
        name="combine",
    )(*(in_vmem(part) for part in parts))


def on_device(
    cells,
    cell_bins,
    tile_counts,
    bin_base,
    norm_gain,
    expert_ids,
    gate_q,
    up_q,
    down_q,
    gate_scales,
    up_scales,
    down_scales,
):
    dp_size = lax.axis_size("dp")
    chips = dp_size // CORES
    expert_count = lax.axis_size("expert") * gate_q.shape[0]
    cell_total, width = cells.shape
    tile_bins = bin_base.shape[0]
    core = (lax.axis_index("dp") % CORES).astype(jnp.int32).reshape(1)
    to_core = [(i, i ^ 1) for i in range(dp_size)]

    def to_chip(k):
        return [(i, (i + CORES * k) % dp_size) for i in range(dp_size)]

    same_core = [[CORES * x + c for x in range(chips)] for c in range(CORES)]

    for_other, own_sums = splat(
        tile_counts, core, cell_bins.reshape(1, cell_total), cells, chips, tile_bins
    )
    sums = join(own_sums, lax.ppermute(for_other, "dp", to_core))
    quants = (gate_q[0], up_q[0], down_q[0])
    *quants, sums = lax.optimization_barrier((*quants, sums))
    got = lax.all_to_all(
        sums,
        "dp",
        split_axis=0,
        concat_axis=0,
        tiled=True,
        axis_index_groups=same_core,
    )
    mine = dequantize_all(quants, (gate_scales[0], up_scales[0], down_scales[0]))
    theirs = [lax.ppermute(w, "dp", to_core) for w in mine]

    capacity = max(2, 3 * tile_bins // (2 * expert_count))
    expert_col = expert_ids[:, 0]
    one_hot = (expert_col[:, None] == jnp.arange(expert_count, dtype=jnp.int32)[None, :]).astype(
        jnp.int32
    )
    within = jnp.sum(jnp.cumsum(one_hot, axis=0) * one_hot, axis=1) - 1
    slot_of = expert_col * capacity + within
    slots = expert_count * capacity
    outgoing, residual_in = route(
        got, bin_base, norm_gain.reshape(1, width), slot_of.reshape(1, tile_bins), slots
    )
    dense = (expert_count, capacity * width // QB, QB)
    arrived = lax.all_to_all(
        outgoing.reshape(dense), "expert", split_axis=0, concat_axis=0, tiled=True
    ).reshape(slots, width)

    others = [(k, lax.ppermute(arrived, "dp", to_chip(k))) for k in (1, chips - 1, *range(2, chips - 1))]
    own, held = load_ffn(arrived, [*mine, *theirs])
    backs = [lax.ppermute(ffn(there, held), "dp", to_chip(chips - k)) for k, there in others]
    returned = lax.all_to_all(
        combine([own, *backs]).reshape(dense), "expert", split_axis=0, concat_axis=0, tiled=True
    ).reshape(slots, width)
    placer = (jnp.arange(slots, dtype=jnp.int32)[:, None] == slot_of[None, :]).astype(jnp.bfloat16)
    expert_out = lax.dot_general(
        placer, returned, (((0,), (0,)), ((), ())), preferred_element_type=jnp.float32
    )
    return (residual_in + expert_out).astype(jnp.bfloat16)


def solution(mesh):
    split = P(("dp", "expert"), None)
    placed = (split, P(("dp", "expert")), split, split, P(), split) + (P("expert", "dp", None),) * 6
    return jax.shard_map(on_device, mesh=mesh, in_specs=placed, out_specs=split, check_vma=False)
```

```python
import jax
import jax.numpy as jnp
from jax import lax
from jax.experimental import pallas as pl
from jax.experimental.pallas import tpu as pltpu
from jax.sharding import PartitionSpec as P

QB = 128
CORES = 2
CHUNK = 256
LIMIT = 8 << 20


def in_vmem(x):
    return pltpu.with_memory_space_constraint(x, pltpu.VMEM)


def in_hbm(x):
    return pltpu.with_memory_space_constraint(x, pltpu.HBM)


def splat_kernel(counts_ref, core_ref, bins_ref, cells_ref, other_ref, own_ref, held, sem):
    copy = pltpu.make_async_copy(cells_ref, held, sem)
    copy.start()
    chips, rows, _ = own_ref.shape
    total = held.shape[0]
    position = lax.broadcasted_iota(jnp.int32, (1, total), 1)
    tile = jnp.zeros((1, total), jnp.int32)
    run_end = jnp.int32(0)
    for k in range(counts_ref.shape[1]):
        run_end = run_end + counts_ref[0, k]
        tile = tile + (position >= run_end).astype(jnp.int32)
    code = tile * rows + bins_ref[...]
    row = lax.broadcasted_iota(jnp.int32, (rows, total), 0)
    copy.wait()
    cells = held[...]
    for core, out_ref in ((1 - core_ref[0], other_ref), (core_ref[0], own_ref)):
        for chip in range(chips):
            match = row + (chip * CORES + core) * rows == code
            out_ref[chip] = jnp.dot(
                match.astype(jnp.float32).astype(jnp.bfloat16), cells, preferred_element_type=jnp.float32
            ).astype(out_ref.dtype)


def splat(counts, core, bins, cells, chips, tile_bins):
    vmem = pl.BlockSpec(memory_space=pltpu.VMEM)
    smem = pl.BlockSpec(memory_space=pltpu.SMEM)
    shape = (chips, tile_bins, cells.shape[1])
    return pl.pallas_call(
        splat_kernel,
        in_specs=[smem, smem, vmem, pl.BlockSpec(memory_space=pltpu.HBM)],
        out_specs=[vmem, vmem],
        out_shape=[pltpu.VMEM(shape, jnp.bfloat16), pltpu.VMEM(shape, jnp.float32)],
        scratch_shapes=[pltpu.VMEM(cells.shape, jnp.bfloat16), pltpu.SemaphoreType.DMA],
        compiler_params=pltpu.CompilerParams(vmem_limit_bytes=LIMIT),
        name="splat",
    )(in_hbm(counts), core, in_hbm(bins), in_hbm(cells))


def join_kernel(own_ref, got_ref, out_ref, sums, sems):
    chips = own_ref.shape[0]
    copies = [pltpu.make_async_copy(sums.at[chip], out_ref.at[chip], sems.at[chip]) for chip in range(chips)]
    for chip in range(chips):
        sums[chip] = (own_ref[chip] + got_ref[chip].astype(jnp.float32)).astype(sums.dtype)
        copies[chip].start()
    for copy in copies:
        copy.wait()


def join(own, got):
    vmem = pl.BlockSpec(memory_space=pltpu.VMEM)
    return pl.pallas_call(
        join_kernel,
        in_specs=[vmem, vmem],
        out_specs=pl.BlockSpec(memory_space=pltpu.HBM),
        out_shape=pltpu.HBM(got.shape, got.dtype),
        scratch_shapes=[pltpu.VMEM(got.shape, got.dtype), pltpu.SemaphoreType.DMA((got.shape[0],))],
        compiler_params=pltpu.CompilerParams(vmem_limit_bytes=LIMIT),
        name="join",
    )(in_vmem(own), in_vmem(got))


def dequant_kernel(gs, us, ds, gq, uq, dq, *outs):
    hidden, width = gq.shape

    def scaled(s_ref, q_ref, row, col):
        block = q_ref[row * QB : (row + 1) * QB, col * QB : (col + 1) * QB]
        exponent = jnp.full((1, QB), s_ref[row, col], jnp.int32)
        return block * jnp.exp2(exponent.astype(jnp.float32)).astype(jnp.bfloat16)

    for row in range(hidden // QB):
        out, at = outs[row * QB // CHUNK], row * QB % CHUNK
        for col in range(width // QB):
            rows, cols = slice(row * QB, (row + 1) * QB), slice(col * QB, (col + 1) * QB)
            out[cols, at : at + QB] = scaled(gs, gq, row, col).T
            out[cols, CHUNK + at : CHUNK + at + QB] = scaled(us, uq, row, col).T
            outs[-1][rows, cols] = scaled(ds, dq, row, col)


def dequantize_all(quants, scales):
    rows, cols = quants[0].shape
    vmem = pl.BlockSpec(memory_space=pltpu.VMEM)
    chunks = rows // CHUNK
    return pl.pallas_call(
        dequant_kernel,
        in_specs=[pl.BlockSpec(memory_space=pltpu.SMEM)] * 3 + [vmem] * 3,
        out_specs=[vmem] * (chunks + 1),
        out_shape=[pltpu.HBM((cols, 2 * CHUNK), jnp.bfloat16)] * chunks
        + [pltpu.HBM((rows, cols), jnp.bfloat16)],
        compiler_params=pltpu.CompilerParams(vmem_limit_bytes=LIMIT),
        name="dequantize",
    )(*scales, *quants)


def route_kernel(got_ref, base_ref, gain_ref, slot_ref, out_ref, residual_ref, spread, kept, sem):
    residual = base_ref[...].astype(jnp.float32)
    for chip in range(got_ref.shape[0]):
        residual = residual + got_ref[chip].astype(jnp.float32)
    kept[...] = residual
    copy = pltpu.make_async_copy(kept, residual_ref, sem)
    copy.start()
    mean_sq = jnp.mean(residual * residual, axis=1, keepdims=True)
    normed = (residual * lax.rsqrt(mean_sq + 1e-06) * gain_ref[...]).astype(jnp.bfloat16)
    bins, width = residual.shape
    slots = out_ref.shape[0] * QB // width
    placer = lax.broadcasted_iota(jnp.int32, (slots, bins), 0) == slot_ref[...]
    placed = jnp.dot(
        placer.astype(jnp.float32).astype(jnp.bfloat16), normed, preferred_element_type=jnp.float32
    )
    spread_rows(placed, spread, out_ref)
    copy.wait()


def route(got, base, gain, slot_of, slots):
    bins, width = base.shape
    rows = slots * width // QB
    vmem = pl.BlockSpec(memory_space=pltpu.VMEM)
    return pl.pallas_call(
        route_kernel,
        in_specs=[vmem] * 4,
        out_specs=[vmem, pl.BlockSpec(memory_space=pltpu.HBM)],
        out_shape=[
            pltpu.VMEM((rows, QB), jnp.bfloat16),
            pltpu.HBM((bins, width), jnp.float32),
        ],
        scratch_shapes=[
            pltpu.VMEM((rows + width // QB, QB), jnp.float32),
            pltpu.VMEM((bins, width), jnp.float32),
            pltpu.SemaphoreType.DMA,
        ],
        compiler_params=pltpu.CompilerParams(vmem_limit_bytes=LIMIT),
        name="route",
    )(in_vmem(got), in_vmem(base), gain, slot_of)


def through_experts(x, weights, wait=None):
    half = len(weights) // 2
    total = None
    for core in range(2):
        first, last = core * half, core * half + half - 1
        for i in range(first, last):
            if wait is not None:
                wait(i)
            both = jnp.dot(x, weights[i][...], preferred_element_type=jnp.float32)
            gate, up = both[:, :CHUNK], both[:, CHUNK:]
            hidden = (gate / (1.0 + jnp.exp(-gate)) * up).astype(jnp.bfloat16)
            if wait is not None and i == first:
                wait(last)
            at = (i - first) * CHUNK
            part = jnp.dot(hidden, weights[last][at : at + CHUNK, :], preferred_element_type=jnp.float32)
            total = part if total is None else total + part
    return total


def load_ffn_kernel(x_ref, *refs):
    count = (len(refs) - 2) // 2
    weights, out_ref, held, sems = refs[:count], refs[count], refs[count + 1 : -1], refs[-1]
    copies = [pltpu.make_async_copy(weights[i], held[i], sems.at[i]) for i in range(count)]
    for copy in copies:
        copy.start()
    out_ref[...] = through_experts(x_ref[...], held, lambda i: copies[i].wait()).astype(out_ref.dtype)


def load_ffn(x, weights):
    vmem = pl.BlockSpec(memory_space=pltpu.VMEM)
    hbm = pl.BlockSpec(memory_space=pltpu.HBM)
    out, *held = pl.pallas_call(
        load_ffn_kernel,
        in_specs=[vmem] + [hbm] * len(weights),
        out_specs=[vmem] * (1 + len(weights)),
        out_shape=[pltpu.VMEM(v.shape, jnp.bfloat16) for v in (x, *weights)],
        scratch_shapes=[pltpu.SemaphoreType.DMA((len(weights),))],
        compiler_params=pltpu.CompilerParams(vmem_limit_bytes=LIMIT),
        name="load_ffn",
    )(in_vmem(x), *(in_hbm(w) for w in weights))
    return out, held


def ffn_kernel(x_ref, *refs):
    *weights, out_ref = refs
    out_ref[...] = through_experts(x_ref[...], weights).astype(out_ref.dtype)


def ffn(x, weights):
    vmem = pl.BlockSpec(memory_space=pltpu.VMEM)
    return pl.pallas_call(
        ffn_kernel,
        in_specs=[vmem] * (1 + len(weights)),
        out_specs=vmem,
        out_shape=pltpu.VMEM(x.shape, jnp.bfloat16),
        compiler_params=pltpu.CompilerParams(vmem_limit_bytes=LIMIT),
        name="ffn",
    )(*(in_vmem(v) for v in (x, *weights)))


def spread_rows(rows, spread, out_ref):
    lanes = rows.shape[1] // QB
    for col in range(lanes):
        spread[pl.ds(col, rows.shape[0], stride=lanes), :] = rows[:, col * QB : (col + 1) * QB]
    out_ref[...] = spread[: out_ref.shape[0], :].astype(out_ref.dtype)


def combine_kernel(*refs):
    *parts, out_ref, spread = refs
    total = parts[0][...].astype(jnp.float32)
    for part in parts[1:]:
        total = total + part[...].astype(jnp.float32)
    spread_rows(total, spread, out_ref)


def combine(parts):
    slots, width = parts[0].shape
    vmem = pl.BlockSpec(memory_space=pltpu.VMEM)
    rows = slots * width // QB
    return pl.pallas_call(
        combine_kernel,
        in_specs=[vmem] * len(parts),
        out_specs=vmem,
        out_shape=pltpu.VMEM((rows, QB), jnp.bfloat16),
        scratch_shapes=[pltpu.VMEM((rows + width // QB, QB), jnp.float32)],
        compiler_params=pltpu.CompilerParams(vmem_limit_bytes=LIMIT),
        name="combine",
    )(*(in_vmem(part) for part in parts))


def on_device(
    cells,
    cell_bins,
    tile_counts,
    bin_base,
    norm_gain,
    expert_ids,
    gate_q,
    up_q,
    down_q,
    gate_scales,
    up_scales,
    down_scales,
):
    dp_size = lax.axis_size("dp")
    chips = dp_size // CORES
    expert_count = lax.axis_size("expert") * gate_q.shape[0]
    cell_total, width = cells.shape
    tile_bins = bin_base.shape[0]
    core = (lax.axis_index("dp") % CORES).astype(jnp.int32).reshape(1)
    to_core = [(i, i ^ 1) for i in range(dp_size)]

    def to_chip(k):
        return [(i, (i + CORES * k) % dp_size) for i in range(dp_size)]

    same_core = [[CORES * x + c for x in range(chips)] for c in range(CORES)]

    for_other, own_sums = splat(
        tile_counts, core, cell_bins.reshape(1, cell_total), cells, chips, tile_bins
    )
    sums = join(own_sums, lax.ppermute(for_other, "dp", to_core))
    quants = (gate_q[0], up_q[0], down_q[0])
    *quants, sums = lax.optimization_barrier((*quants, sums))
    got = lax.all_to_all(
        sums,
        "dp",
        split_axis=0,
        concat_axis=0,
        tiled=True,
        axis_index_groups=same_core,
    )
    mine = dequantize_all(quants, (gate_scales[0], up_scales[0], down_scales[0]))
    theirs = [lax.ppermute(w, "dp", to_core) for w in mine]

    capacity = max(2, 3 * tile_bins // (2 * expert_count))
    expert_col = expert_ids[:, 0]
    one_hot = (expert_col[:, None] == jnp.arange(expert_count, dtype=jnp.int32)[None, :]).astype(
        jnp.int32
    )
    within = jnp.sum(jnp.cumsum(one_hot, axis=0) * one_hot, axis=1) - 1
    slot_of = expert_col * capacity + within
    slots = expert_count * capacity
    outgoing, residual_in = route(
        got, bin_base, norm_gain.reshape(1, width), slot_of.reshape(1, tile_bins), slots
    )
    dense = (expert_count, capacity * width // QB, QB)
    arrived = lax.all_to_all(
        outgoing.reshape(dense), "expert", split_axis=0, concat_axis=0, tiled=True
    ).reshape(slots, width)

    others = [(k, lax.ppermute(arrived, "dp", to_chip(k))) for k in (1, chips - 1, *range(2, chips - 1))]
    own, held = load_ffn(arrived, [*mine, *theirs])
    backs = [lax.ppermute(ffn(there, held), "dp", to_chip(chips - k)) for k, there in others]
    returned = lax.all_to_all(
        combine([own, *backs]).reshape(dense), "expert", split_axis=0, concat_axis=0, tiled=True
    ).reshape(slots, width)
    placer = (jnp.arange(slots, dtype=jnp.int32)[:, None] == slot_of[None, :]).astype(jnp.bfloat16)
    expert_out = lax.dot_general(
        placer, returned, (((0,), (0,)), ((), ())), preferred_element_type=jnp.float32
    )
    return (residual_in + expert_out).astype(jnp.bfloat16)


def solution(mesh):
    split = P(("dp", "expert"), None)
    placed = (split, P(("dp", "expert")), split, split, P(), split) + (P("expert", "dp", None),) * 6
    return jax.shard_map(on_device, mesh=mesh, in_specs=placed, out_specs=split, check_vma=False)
```

```python
import jax
import jax.numpy as jnp
from jax import lax
from jax.experimental import pallas as pl
from jax.experimental.pallas import tpu as pltpu
from jax.sharding import PartitionSpec as P

QB = 128
CORES = 2
CHUNK = 256
GROUPS = 4
LIMIT = 8 << 20


def in_vmem(x):
    return pltpu.with_memory_space_constraint(x, pltpu.VMEM)


def in_hbm(x):
    return pltpu.with_memory_space_constraint(x, pltpu.HBM)


def splat_kernel(counts_ref, core_ref, bins_ref, cells_ref, other_ref, own_ref, held, sem):
    copy = pltpu.make_async_copy(cells_ref, held, sem)
    copy.start()
    chips, rows, _ = own_ref.shape
    total = held.shape[0]
    position = lax.broadcasted_iota(jnp.int32, (1, total), 1)
    tile = jnp.zeros((1, total), jnp.int32)
    run_end = jnp.int32(0)
    for k in range(counts_ref.shape[1]):
        run_end = run_end + counts_ref[0, k]
        tile = tile + (position >= run_end).astype(jnp.int32)
    code = tile * rows + bins_ref[...]
    row = lax.broadcasted_iota(jnp.int32, (rows, total), 0)
    copy.wait()
    cells = held[...]
    for core, out_ref in ((1 - core_ref[0], other_ref), (core_ref[0], own_ref)):
        for chip in range(chips):
            match = row + (chip * CORES + core) * rows == code
            out_ref[chip] = jnp.dot(
                match.astype(jnp.float32).astype(jnp.bfloat16), cells, preferred_element_type=jnp.float32
            ).astype(out_ref.dtype)


def splat(counts, core, bins, cells, chips, tile_bins):
    vmem = pl.BlockSpec(memory_space=pltpu.VMEM)
    smem = pl.BlockSpec(memory_space=pltpu.SMEM)
    shape = (chips, tile_bins, cells.shape[1])
    return pl.pallas_call(
        splat_kernel,
        in_specs=[smem, smem, vmem, pl.BlockSpec(memory_space=pltpu.HBM)],
        out_specs=[vmem, vmem],
        out_shape=[pltpu.VMEM(shape, jnp.bfloat16), pltpu.VMEM(shape, jnp.float32)],
        scratch_shapes=[pltpu.VMEM(cells.shape, jnp.bfloat16), pltpu.SemaphoreType.DMA],
        compiler_params=pltpu.CompilerParams(vmem_limit_bytes=LIMIT),
        name="splat",
    )(in_hbm(counts), core, in_hbm(bins), in_hbm(cells))


def join_kernel(own_ref, got_ref, out_ref, sums, sems):
    chips = own_ref.shape[0]
    copies = [pltpu.make_async_copy(sums.at[chip], out_ref.at[chip], sems.at[chip]) for chip in range(chips)]
    for chip in range(chips):
        sums[chip] = (own_ref[chip] + got_ref[chip].astype(jnp.float32)).astype(sums.dtype)
        copies[chip].start()
    for copy in copies:
        copy.wait()


def join(own, got):
    vmem = pl.BlockSpec(memory_space=pltpu.VMEM)
    return pl.pallas_call(
        join_kernel,
        in_specs=[vmem, vmem],
        out_specs=pl.BlockSpec(memory_space=pltpu.HBM),
        out_shape=pltpu.HBM(got.shape, got.dtype),
        scratch_shapes=[pltpu.VMEM(got.shape, got.dtype), pltpu.SemaphoreType.DMA((got.shape[0],))],
        compiler_params=pltpu.CompilerParams(vmem_limit_bytes=LIMIT),
        name="join",
    )(in_vmem(own), in_vmem(got))


def dequant_kernel(gs, us, ds, gq, uq, dq, *outs):
    hidden, width = gq.shape

    def scaled(s_ref, q_ref, row, col):
        block = q_ref[row * QB : (row + 1) * QB, col * QB : (col + 1) * QB]
        exponent = jnp.full((1, QB), s_ref[row, col], jnp.int32)
        return block * jnp.exp2(exponent.astype(jnp.float32)).astype(jnp.bfloat16)

    for row in range(hidden // QB):
        out, at = outs[row * QB // CHUNK], row * QB % CHUNK
        for col in range(width // QB):
            rows, cols = slice(row * QB, (row + 1) * QB), slice(col * QB, (col + 1) * QB)
            out[cols, at : at + QB] = scaled(gs, gq, row, col).T
            out[cols, CHUNK + at : CHUNK + at + QB] = scaled(us, uq, row, col).T
            outs[-1][rows, cols] = scaled(ds, dq, row, col)


def dequantize_all(quants, scales):
    rows, cols = quants[0].shape
    vmem = pl.BlockSpec(memory_space=pltpu.VMEM)
    chunks = rows // CHUNK
    return pl.pallas_call(
        dequant_kernel,
        in_specs=[pl.BlockSpec(memory_space=pltpu.SMEM)] * 3 + [vmem] * 3,
        out_specs=[vmem] * (chunks + 1),
        out_shape=[pltpu.HBM((cols, 2 * CHUNK), jnp.bfloat16)] * chunks
        + [pltpu.HBM((rows, cols), jnp.bfloat16)],
        compiler_params=pltpu.CompilerParams(vmem_limit_bytes=LIMIT),
        name="dequantize",
    )(*scales, *quants)


def route_kernel(got_ref, base_ref, gain_ref, slot_ref, out_ref, residual_ref, spread, packed, sems, kept, sem):
    residual = base_ref[...].astype(jnp.float32)
    for chip in range(got_ref.shape[0]):
        residual = residual + got_ref[chip].astype(jnp.float32)
    kept[...] = residual
    copy = pltpu.make_async_copy(kept, residual_ref, sem)
    copy.start()
    mean_sq = jnp.mean(residual * residual, axis=1, keepdims=True)
    normed = (residual * lax.rsqrt(mean_sq + 1e-06) * gain_ref[...]).astype(jnp.bfloat16)
    bins, width = residual.shape
    slots = out_ref.shape[0] * QB // width
    placer = lax.broadcasted_iota(jnp.int32, (slots, bins), 0) == slot_ref[...]
    placed = jnp.dot(
        placer.astype(jnp.float32).astype(jnp.bfloat16), normed, preferred_element_type=jnp.float32
    )
    count = slots // GROUPS
    spread_rows(lambda g: placed[g * count : (g + 1) * count], spread, packed, out_ref, sems)
    copy.wait()


def route(got, base, gain, slot_of, slots):
    bins, width = base.shape
    rows = slots * width // QB
    vmem = pl.BlockSpec(memory_space=pltpu.VMEM)
    return pl.pallas_call(
        route_kernel,
        in_specs=[vmem] * 4,
        out_specs=[pl.BlockSpec(memory_space=pltpu.HBM)] * 2,
        out_shape=[
            pltpu.HBM((rows, QB), jnp.bfloat16),
            pltpu.HBM((bins, width), jnp.float32),
        ],
        scratch_shapes=spread_scratch(rows, width)
        + [
            pltpu.VMEM((bins, width), jnp.float32),
            pltpu.SemaphoreType.DMA,
        ],
        compiler_params=pltpu.CompilerParams(vmem_limit_bytes=LIMIT),
        name="route",
    )(in_vmem(got), in_vmem(base), gain, slot_of)


def through_experts(x, weights, wait=None):
    half = len(weights) // 2
    total = None
    for core in range(2):
        first, last = core * half, core * half + half - 1
        for i in range(first, last):
            if wait is not None:
                wait(i)
            both = jnp.dot(x, weights[i][...], preferred_element_type=jnp.float32)
            gate, up = both[:, :CHUNK], both[:, CHUNK:]
            hidden = (gate / (1.0 + jnp.exp(-gate)) * up).astype(jnp.bfloat16)
            if wait is not None and i == first:
                wait(last)
            at = (i - first) * CHUNK
            part = jnp.dot(hidden, weights[last][at : at + CHUNK, :], preferred_element_type=jnp.float32)
            total = part if total is None else total + part
    return total


def load_ffn_kernel(x_ref, *refs):
    count = (len(refs) - 2) // 2
    weights, out_ref, held, sems = refs[:count], refs[count], refs[count + 1 : -1], refs[-1]
    copies = [pltpu.make_async_copy(weights[i], held[i], sems.at[i]) for i in range(count)]
    for copy in copies:
        copy.start()
    out_ref[...] = through_experts(x_ref[...], held, lambda i: copies[i].wait()).astype(out_ref.dtype)


def load_ffn(x, weights):
    vmem = pl.BlockSpec(memory_space=pltpu.VMEM)
    hbm = pl.BlockSpec(memory_space=pltpu.HBM)
    out, *held = pl.pallas_call(
        load_ffn_kernel,
        in_specs=[vmem] + [hbm] * len(weights),
        out_specs=[vmem] * (1 + len(weights)),
        out_shape=[pltpu.VMEM(v.shape, jnp.bfloat16) for v in (x, *weights)],
        scratch_shapes=[pltpu.SemaphoreType.DMA((len(weights),))],
        compiler_params=pltpu.CompilerParams(vmem_limit_bytes=LIMIT),
        name="load_ffn",
    )(in_vmem(x), *(in_hbm(w) for w in weights))
    return out, held


def ffn_kernel(x_ref, *refs):
    *weights, out_ref = refs
    out_ref[...] = through_experts(x_ref[...], weights).astype(out_ref.dtype)


def ffn(x, weights):
    vmem = pl.BlockSpec(memory_space=pltpu.VMEM)
    return pl.pallas_call(
        ffn_kernel,
        in_specs=[vmem] * (1 + len(weights)),
        out_specs=vmem,
        out_shape=pltpu.VMEM(x.shape, jnp.bfloat16),
        compiler_params=pltpu.CompilerParams(vmem_limit_bytes=LIMIT),
        name="ffn",
    )(*(in_vmem(v) for v in (x, *weights)))


def spread_rows(rows_of, spread, packed, out_ref, sems):
    copies = []
    for group in range(GROUPS):
        rows = rows_of(group)
        count, lanes = rows.shape[0], rows.shape[1] // QB
        for col in range(lanes):
            spread[group, pl.ds(col, count, stride=lanes), :] = rows[:, col * QB : (col + 1) * QB]
        packed[group] = spread[group, : count * lanes, :].astype(packed.dtype)
        at = pl.ds(group * count * lanes, count * lanes)
        copies.append(pltpu.make_async_copy(packed.at[group], out_ref.at[at], sems.at[group]))
        copies[-1].start()
    for copy in copies:
        copy.wait()


def spread_scratch(rows, width):
    return [
        pltpu.VMEM((GROUPS, rows // GROUPS + width // QB, QB), jnp.float32),
        pltpu.VMEM((GROUPS, rows // GROUPS, QB), jnp.bfloat16),
        pltpu.SemaphoreType.DMA((GROUPS,)),
    ]


def combine_kernel(*refs):
    *parts, out_ref, spread, packed, sems = refs
    count = parts[0].shape[0] // GROUPS

    def rows_of(group):
        at = slice(group * count, (group + 1) * count)
        total = parts[0][at, :].astype(jnp.float32)
        for part in parts[1:]:
            total = total + part[at, :].astype(jnp.float32)
        return total

    spread_rows(rows_of, spread, packed, out_ref, sems)


def combine(parts):
    slots, width = parts[0].shape
    vmem = pl.BlockSpec(memory_space=pltpu.VMEM)
    rows = slots * width // QB
    return pl.pallas_call(
        combine_kernel,
        in_specs=[vmem] * len(parts),
        out_specs=pl.BlockSpec(memory_space=pltpu.HBM),
        out_shape=pltpu.HBM((rows, QB), jnp.bfloat16),
        scratch_shapes=spread_scratch(rows, width),
        compiler_params=pltpu.CompilerParams(vmem_limit_bytes=LIMIT),
        name="combine",
    )(*(in_vmem(part) for part in parts))


def on_device(
    cells,
    cell_bins,
    tile_counts,
    bin_base,
    norm_gain,
    expert_ids,
    gate_q,
    up_q,
    down_q,
    gate_scales,
    up_scales,
    down_scales,
):
    dp_size = lax.axis_size("dp")
    chips = dp_size // CORES
    expert_count = lax.axis_size("expert") * gate_q.shape[0]
    cell_total, width = cells.shape
    tile_bins = bin_base.shape[0]
    core = (lax.axis_index("dp") % CORES).astype(jnp.int32).reshape(1)
    to_core = [(i, i ^ 1) for i in range(dp_size)]

    def to_chip(k):
        return [(i, (i + CORES * k) % dp_size) for i in range(dp_size)]

    same_core = [[CORES * x + c for x in range(chips)] for c in range(CORES)]

    for_other, own_sums = splat(
        tile_counts, core, cell_bins.reshape(1, cell_total), cells, chips, tile_bins
    )
    sums = join(own_sums, lax.ppermute(for_other, "dp", to_core))
    quants = (gate_q[0], up_q[0], down_q[0])
    *quants, sums = lax.optimization_barrier((*quants, sums))
    got = lax.all_to_all(
        sums,
        "dp",
        split_axis=0,
        concat_axis=0,
        tiled=True,
        axis_index_groups=same_core,
    )
    mine = dequantize_all(quants, (gate_scales[0], up_scales[0], down_scales[0]))
    theirs = [lax.ppermute(w, "dp", to_core) for w in mine]

    capacity = max(2, 3 * tile_bins // (2 * expert_count))
    expert_col = expert_ids[:, 0]
    one_hot = (expert_col[:, None] == jnp.arange(expert_count, dtype=jnp.int32)[None, :]).astype(
        jnp.int32
    )
    within = jnp.sum(jnp.cumsum(one_hot, axis=0) * one_hot, axis=1) - 1
    slot_of = expert_col * capacity + within
    slots = expert_count * capacity
    outgoing, residual_in = route(
        got, bin_base, norm_gain.reshape(1, width), slot_of.reshape(1, tile_bins), slots
    )
    dense = (expert_count, capacity * width // QB, QB)
    arrived = lax.all_to_all(
        outgoing.reshape(dense), "expert", split_axis=0, concat_axis=0, tiled=True
    ).reshape(slots, width)

    others = [(k, lax.ppermute(arrived, "dp", to_chip(k))) for k in (1, chips - 1, *range(2, chips - 1))]
    own, held = load_ffn(arrived, [*mine, *theirs])
    backs = [lax.ppermute(ffn(there, held), "dp", to_chip(chips - k)) for k, there in others]
    returned = lax.all_to_all(
        combine([own, *backs]).reshape(dense), "expert", split_axis=0, concat_axis=0, tiled=True
    ).reshape(slots, width)
    placer = (jnp.arange(slots, dtype=jnp.int32)[:, None] == slot_of[None, :]).astype(jnp.bfloat16)
    expert_out = lax.dot_general(
        placer, returned, (((0,), (0,)), ((), ())), preferred_element_type=jnp.float32
    )
    return (residual_in + expert_out).astype(jnp.bfloat16)


def solution(mesh):
    split = P(("dp", "expert"), None)
    placed = (split, P(("dp", "expert")), split, split, P(), split) + (P("expert", "dp", None),) * 6
    return jax.shard_map(on_device, mesh=mesh, in_specs=placed, out_specs=split, check_vma=False)
```
